512 devices in a mesh: tm: 16 (over y_lo, z), space: 32 (over x, y_hi, core).
Axes of the slice: x: 4, y: 8 (y_hi: 4, y_lo: 2; y = y_hi * 2 + y_lo), z: 8, core: 2. Of those that a mesh axis runs over, the one named last changes fastest.
Arguments:
- region_map: int32 [256, 128, 128], P('space'), may hold values from 0 to 7
- region_coef: float32 [8], replicated, may hold values from 0.08 to 0.32
- source_cell: int32 [32768], P('space'), may hold values from 0 to 131071
- amplitude: float32 [16, 8, 32768], P('tm', None, 'space'), may hold values from -4 to 4
Outputs:
- states: float32 [16, 2, 256, 128, 128], P('tm', None, 'space')
The draws below stay inside these ranges and needn't reach their ends.
All inputs are finite; a program needn't handle non-finite values.
Results may differ from the reference program's by a relative error of at most 0.00002.
Values sent between devices are 32-bit elements; how exact they have to be, the bound alone decides.
A program may use at most 64 MiB of HBM per device.

```python
import math
import jax
import jax.numpy as jnp
from jax import lax

CZ = 8
NX = 128
NY = 128
SRC_DEV = 1024
REGIONS = 8
STEPS = 8
SPAN = 3
WIN = 16
NZ = 256
SOURCES = 32768


def place_ends(entries, stream_key, least, largest):
    extent = entries.shape
    place = [jax.random.randint(jax.random.fold_in(stream_key, axis), (), 0, extent[axis]) for axis in range(len(extent))]
    entries = entries.at[tuple(place)].set(least)
    longest = extent.index(max(extent))
    place[longest] = (place[longest] + 1) % extent[longest]
    return entries.at[tuple(place)].set(largest)


def shard_levels(rng, shape, cuts, smallest, high):
    def one(position, blocks):
        steps = jax.random.uniform(jax.random.fold_in(jax.random.fold_in(rng, 6), position), (blocks,), jnp.float32, smallest / len(cuts), high / len(cuts))
        return jnp.repeat(jnp.exp(steps), shape[position] // blocks).reshape((-1,) + (1,) * (len(shape) - position - 1))

    factor_of = one(*cuts[0])
    for cut in cuts[1:]:
        factor_of = factor_of * one(*cut)
    return factor_of


def noise(stream_key, shape, width, most, shards=(), kind=jnp.bfloat16):
    loudness = shard_levels(stream_key, shape, shards, -0.22, 0.18) if shards else 1.0
    result = jax.random.normal(stream_key, shape, jnp.float32) * width * loudness
    return jnp.minimum(jnp.maximum(result, -most), most).astype(kind)


def setup_inputs(seed: int = 0) -> dict:
    keys = jax.random.split(jax.random.key(seed), 5)
    region_map = place_ends(jax.random.randint(keys[0], (NZ, NX, NY), 0, REGIONS), jax.random.fold_in(keys[0], 1), 0, REGIONS - 1).astype(jnp.int32)
    region_coef = jnp.clip(jnp.exp(jax.random.uniform(keys[1], (REGIONS,), jnp.float32, math.log(0.08), math.log(0.32))), 0.08, 0.32)
    source_cell = place_ends(jax.random.randint(keys[2], (SOURCES,), 0, CZ * NX * NY), jax.random.fold_in(keys[2], 1), 0, (CZ * NX * NY) - 1).astype(jnp.int32)
    amplitude = noise(keys[3], (WIN, STEPS, SOURCES), 0.5, 4.0, ((0, 16), (2, 32)), jnp.float32)
    return dict(region_map=region_map, region_coef=region_coef, source_cell=source_cell, amplitude=amplitude)


def laplace(field):
    padded = jnp.pad(field, 1)
    beside = padded[2:, 1:-1, 1:-1] + padded[:-2, 1:-1, 1:-1]
    beside = beside + padded[1:-1, 2:, 1:-1] + padded[1:-1, :-2, 1:-1]
    beside = beside + padded[1:-1, 1:-1, 2:] + padded[1:-1, 1:-1, :-2]
    return beside - 6.0 * field


def leap_step(carried_pair, courant, forcing):
    earlier, current = carried_pair
    newest = 2.0 * current - earlier + courant * laplace(current) + forcing
    return (current, newest)


def reference(region_map, region_coef, source_cell, amplitude):
    courant = region_coef[region_map]
    slab_cells = CZ * NX * NY
    owner_start = (jnp.arange(SOURCES, dtype=jnp.int32) // SRC_DEV) * slab_cells
    global_cell = (owner_start + source_cell).astype(jnp.int32)
    zero_field = jnp.zeros((NZ, NX, NY), jnp.float32)

    def forced(wavelets):
        def advance(which_step, carried_pair):
            forcing = jnp.zeros((NZ * NX * NY,), jnp.float32).at[global_cell].add(wavelets[which_step])
            return leap_step(carried_pair, courant, forcing.reshape(NZ, NX, NY))
        earlier, current = lax.fori_loop(0, STEPS, advance, (zero_field, zero_field))
        return jnp.stack([earlier, current])

    def homogeneous(stacked):
        def advance(which_step, carried_pair):
            return leap_step(carried_pair, courant, zero_field)
        earlier, current = lax.fori_loop(0, STEPS, advance, (stacked[0], stacked[1]))
        return jnp.stack([earlier, current])

    own_states = lax.map(forced, amplitude)
    summed = own_states
    moving = own_states
    for hops in range(1, SPAN + 1):
        moving = lax.map(homogeneous, moving)
        summed = summed.at[hops:].add(moving[:WIN - hops])
    return summed
```

```python
import functools

import jax
import jax.numpy as jnp
from jax import lax
from jax.experimental import pallas as pl
from jax.experimental.pallas import tpu as pltpu
from jax.sharding import PartitionSpec as P

MESH = pl.DeviceIdType.MESH
STEPS = 8
SPAN = 3
ROUNDS = SPAN + 1
GHOST = 4
PIECES = 3
ROW0 = 8


def kernel(
    tms, spaces,
    region_ref, coef_ref, cell_ref, amp_ref, out_ref,
    u, v, co, hist, send, force, rows_hot, cols_hot, amps, pieces,
    amp_send, amp_recv, co_send, co_recv, plane_send, plane_recv,
):
    t, s = lax.axis_index("tm"), lax.axis_index("space")
    cz, nx, ny = region_ref.shape
    own = GHOST + 1
    has = (s > 0, s < spaces - 1)
    beside = ({"space": s - 1}, {"space": s + 1})

    barrier = pltpu.get_barrier_semaphore()
    expected = 0
    partners = [(has[0], beside[0]), (has[1], beside[1])]
    for m in range(1, SPAN + 1):
        partners.append((t - m >= 0, {"tm": t - m}))
        partners.append((t + m < tms, {"tm": t + m}))
    for there, device in partners:
        @pl.when(there)
        def _(device=device):
            pl.semaphore_signal(barrier, inc=1, device_id=device, device_id_type=MESH)
        expected = expected + jnp.where(there, 1, 0)

    def courant_plane(z, _):
        region = region_ref[z]
        value = jnp.zeros((nx, ny), jnp.float32)
        for i in range(coef_ref.shape[0]):
            value = jnp.where(region == i, coef_ref[i], value)
        co[own + z] = value
        return 0

    lax.fori_loop(0, cz, courant_plane, 0)
    zero_plane = jnp.zeros((nx, ny), jnp.float32)

    def clear_u(p, _):
        for i in range(2):
            u[i, p] = jnp.zeros(u.shape[2:], jnp.float32)
        return 0

    def clear_v(z, _):
        for i in range(2):
            v[i, z] = jnp.zeros(v.shape[2:], jnp.float32)
        return 0

    lax.fori_loop(0, u.shape[1], clear_u, 0)
    lax.fori_loop(0, cz, clear_v, 0)
    for m in range(1, SPAN + 1):
        @pl.when(t - m < 0)
        def _(m=m):
            amps[m - 1] = jnp.zeros(amps.shape[1:], jnp.float32)
    for side in range(2):
        @pl.when(jnp.logical_not(has[side]))
        def _(side=side):
            for d in range(GHOST):
                co[own - 1 - d if side == 0 else own + cz + d] = zero_plane

            def clear_hist(i, _):
                hist[i // STEPS, lax.rem(i, STEPS), side] = zero_plane
                return 0

            lax.fori_loop(0, ROUNDS * STEPS, clear_hist, 0)

    pl.semaphore_wait(barrier, expected)

    def amp_copy(m):
        return pltpu.make_async_remote_copy(
            amp_ref.at[0], amps.at[m - 1], amp_send.at[m - 1], amp_recv.at[m - 1],
            device_id={"tm": t + m}, device_id_type=MESH)

    for m in range(SPAN, 0, -1):
        @pl.when(t + m < tms)
        def _(m=m):
            amp_copy(m).start()

    def co_copy(side, d):
        source = own + d if side == 0 else own + cz - 1 - d
        target = own + cz + d if side == 0 else own - 1 - d
        return pltpu.make_async_remote_copy(
            co.at[source], co.at[target], co_send.at[side, d], co_recv.at[1 - side, d],
            device_id=beside[side], device_id_type=MESH)

    def co_wait(side, d):
        target = own - 1 - d if side == 0 else own + cz + d
        return pltpu.make_async_remote_copy(
            co.at[target], co.at[target], co_send.at[side, d], co_recv.at[side, d],
            device_id=beside[side], device_id_type=MESH)

    for d in range(GHOST):
        for side in range(2):
            @pl.when(has[side])
            def _(side=side, d=d):
                co_copy(side, d).start()

    def plane_copy(r, k, side):
        return pltpu.make_async_remote_copy(
            send.at[r, k, side], hist.at[r, k, 1 - side], plane_send.at[r, k, side], plane_recv.at[r, k, 1 - side],
            device_id=beside[side], device_id_type=MESH)

    def plane_wait(r, k, side):
        return pltpu.make_async_remote_copy(
            send.at[r, k, side], hist.at[r, k, side], plane_send.at[r, k, side], plane_recv.at[r, k, side],
            device_id=beside[side], device_id_type=MESH)

    def send_planes(r, k):
        for side in range(2):
            @pl.when(has[side])
            def _(side=side):
                plane_copy(r, k, side).start()

    def await_planes(r, k):
        for side in range(2):
            @pl.when(has[side])
            def _(side=side):
                plane_wait(r, k, side).wait_recv()

    def rows_block(i, _):
        cell = cell_ref[...]
        row = cell // ny
        rows = 64
        index = lax.broadcasted_iota(jnp.int32, (rows, cell.shape[1]), 0) + i * rows
        rows_hot[pl.ds(pl.multiple_of(i * rows, rows), rows), :] = jnp.where(row == index, 1.0, 0.0).astype(jnp.bfloat16)
        return 0

    lax.fori_loop(0, cz * nx // 64, rows_block, 0)

    def cols_block(i, _):
        col = lax.rem(cell_ref[...], ny)
        rows = 64
        index = lax.broadcasted_iota(jnp.int32, (rows, col.shape[1]), 0) + i * rows
        cols_hot[pl.ds(pl.multiple_of(i * rows, rows), rows), :] = jnp.where(col == index, 1.0, 0.0).astype(jnp.bfloat16)
        return 0

    lax.fori_loop(0, ny // 64, cols_block, 0)

    def split_amplitude(slot, value):
        for piece in range(PIECES):
            part = value.astype(jnp.bfloat16)
            pieces[slot, piece] = part.astype(jnp.float32)
            value = value - part.astype(jnp.float32)

    def make_force(slot, n):
        weights = []
        for piece in range(PIECES):
            a = pieces[slot, piece, pl.ds(n, 1), :].astype(jnp.bfloat16)
            weights.append(cols_hot[...] * a)

        rows = 256

        def block(i, _):
            at = pl.ds(pl.multiple_of(i * rows, rows), rows)
            hot = rows_hot[at, :]
            total = None
            for w in weights:
                part = lax.dot_general(hot, w, (((1,), (1,)), ((), ())), preferred_element_type=jnp.float32)
                total = part if total is None else total + part
            force[n, at, :] = total
            return 0

        lax.fori_loop(0, cz * nx // rows, block, 0)

    lane = lax.broadcasted_iota(jnp.int32, (8, ny), 1)
    first_lane, last_lane = lane == 0, lane == ny - 1

    def stencil(c, above, below, up, down, earlier, speed):
        left = jnp.where(first_lane, 0.0, pltpu.roll(c, 1, axis=1))
        right = jnp.where(last_lane, 0.0, pltpu.roll(c, ny - 1, axis=1))
        around = (above + below) + (up + down) + (left + right)
        return (c + c) - earlier + speed * (around - 6.0 * c)

    def run_alone(r, k):
        now, later = (k - 1) % 2, k % 2
        depth = min(k, STEPS - k)

        def block(i, _):
            x = pl.multiple_of(i * 8, 8)
            rows = pl.ds(x + ROW0, 8)
            before = u[now, own - depth - 1, rows, :]
            c = u[now, own - depth, rows, :]
            for z in range(-depth, cz + depth):
                p = own + z
                after = u[now, p + 1, rows, :]
                new = stencil(
                    c, before, after,
                    u[now, p, pl.ds(x + ROW0 - 1, 8), :], u[now, p, pl.ds(x + ROW0 + 1, 8), :],
                    u[later, p, rows, :], co[p, pl.ds(x, 8), :])
                if 0 <= z < cz:
                    new = new + force[k - 1, pl.ds(z * nx + x, 8), :]
                u[later, p, rows, :] = new
                if k < STEPS and z == 0:
                    send[r, k, 0, pl.ds(x, 8), :] = new
                if k < STEPS and z == cz - 1:
                    send[r, k, 1, pl.ds(x, 8), :] = new
                before, c = c, after
            return 0

        lax.fori_loop(0, nx // 8, block, 0)

    def run_caused(r, k):
        now, later = (k - 1) % 2, k % 2
        if k < cz // 2:
            groups = [range(0, k), range(cz - k, cz)]
        else:
            groups = [range(0, cz)]

        def block(i, _):
            x = pl.multiple_of(i * 8, 8)
            rows = pl.ds(x + ROW0, 8)
            at = pl.ds(x, 8)

            def plane(z):
                if z < 0:
                    return hist[r, k - 1, 0, at, :]
                if z >= cz:
                    return hist[r, k - 1, 1, at, :]
                return v[now, z, rows, :]

            for group in groups:
                before, c = plane(group[0] - 1), plane(group[0])
                for z in group:
                    after = plane(z + 1)
                    new = stencil(
                        c, before, after,
                        v[now, z, pl.ds(x + ROW0 - 1, 8), :], v[now, z, pl.ds(x + ROW0 + 1, 8), :],
                        v[later, z, rows, :], co[own + z, at, :])
                    if k < STEPS:
                        v[later, z, rows, :] = new
                    if k >= STEPS - 1:
                        whole = u[later, own + z, rows, :] + new
                        u[later, own + z, rows, :] = whole
                        if k == STEPS and z in (0, cz - 1):
                            side = 0 if z == 0 else 1
                            send[lax.rem(r + 1, ROUNDS), 0, side, at, :] = whole
                    before, c = c, after
            return 0

        lax.fori_loop(0, nx // 8, block, 0)

    for m in range(SPAN, 0, -1):
        @pl.when(t - m >= 0)
        def _(m=m):
            amp_copy(m).wait_recv()
        split_amplitude(SPAN - m, amps[m - 1])
    split_amplitude(SPAN, amp_ref[0])

    def one_round(r, _):
        @pl.when(r > 0)
        def _():
            send_planes(r, 0)

            def clear(d, _):
                for i in range(2):
                    u[i, own - 1 - d] = jnp.zeros(u.shape[2:], jnp.float32)
                    u[i, own + cz + d] = jnp.zeros(u.shape[2:], jnp.float32)
                return 0

            lax.fori_loop(0, GHOST, clear, 0)
            lax.fori_loop(0, cz, clear_v, 0)

        for k in range(1, STEPS + 1):
            @pl.when(r == 0)
            def _(k=k):
                make_force(0, k - 1)
                if k <= GHOST:
                    for side in range(2):
                        @pl.when(has[side])
                        def _(side=side):
                            co_wait(side, k - 1).wait_recv()

            run_alone(r, k)
            if k < STEPS:
                send_planes(r, k)
        for k in range(1, STEPS + 1):
            if k == 1:
                @pl.when(r > 0)
                def _():
                    await_planes(r, 0)
                    run_caused(r, 1)
            else:
                await_planes(r, k - 1)
                run_caused(r, k)

            @pl.when(r < SPAN)
            def _(k=k):
                make_force(r + 1, k - 1)
        return 0

    lax.fori_loop(0, ROUNDS, one_round, 0)

    for i in range(2):
        def copy_out(z, _):
            out_ref[0, i, z] = u[1 - i, own + z, ROW0:ROW0 + nx, :]
            return 0
        lax.fori_loop(0, cz, copy_out, 0)

    for m in range(1, SPAN + 1):
        @pl.when(t + m < tms)
        def _(m=m):
            amp_copy(m).wait_send()
    for side in range(2):
        @pl.when(has[side])
        def _(side=side):
            for d in range(GHOST):
                co_copy(side, d).wait_send()

            def drain(i, _):
                plane_copy(i // STEPS, lax.rem(i, STEPS), side).wait_send()
                return 0

            lax.fori_loop(1, ROUNDS * STEPS, drain, 0)


def solution(mesh):
    tms, spaces = mesh.shape["tm"], mesh.shape["space"]

    def shards(region_map, region_coef, source_cell, amplitude):
        cz, nx, ny = region_map.shape
        sources = source_cell.shape[0]
        planes = cz + 2 * GHOST + 2
        return pl.pallas_call(
            functools.partial(kernel, tms, spaces),
            out_shape=jax.ShapeDtypeStruct((1, 2, cz, nx, ny), jnp.float32),
            in_specs=[
                pl.BlockSpec(memory_space=pltpu.VMEM),
                pl.BlockSpec(memory_space=pltpu.SMEM),
                pl.BlockSpec(memory_space=pltpu.VMEM),
                pl.BlockSpec(memory_space=pltpu.VMEM),
            ],
            out_specs=pl.BlockSpec(memory_space=pltpu.VMEM),
            scratch_shapes=[
                pltpu.VMEM((2, planes, nx + 2 * ROW0, ny), jnp.float32),
                pltpu.VMEM((2, cz, nx + 2 * ROW0, ny), jnp.float32),
                pltpu.VMEM((planes, nx, ny), jnp.float32),
                pltpu.VMEM((ROUNDS, STEPS, 2, nx, ny), jnp.float32),
                pltpu.VMEM((ROUNDS, STEPS, 2, nx, ny), jnp.float32),
                pltpu.VMEM((STEPS, cz * nx, ny), jnp.float32),
                pltpu.VMEM((cz * nx, sources), jnp.bfloat16),
                pltpu.VMEM((ny, sources), jnp.bfloat16),
                pltpu.VMEM((SPAN, STEPS, sources), jnp.float32),
                pltpu.VMEM((ROUNDS, PIECES, STEPS, sources), jnp.float32),
                pltpu.SemaphoreType.DMA((SPAN,)),
                pltpu.SemaphoreType.DMA((SPAN,)),
                pltpu.SemaphoreType.DMA((2, GHOST)),
                pltpu.SemaphoreType.DMA((2, GHOST)),
                pltpu.SemaphoreType.DMA((ROUNDS, STEPS, 2)),
                pltpu.SemaphoreType.DMA((ROUNDS, STEPS, 2)),
            ],
            compiler_params=pltpu.CompilerParams(
                collective_id=0, has_side_effects=True, vmem_limit_bytes=60 << 20
            ),
        )(region_map, region_coef, source_cell.reshape(1, sources), amplitude)

    placed = (P("space", None, None), P(), P("space"), P("tm", None, "space"))
    return jax.shard_map(
        shards, mesh=mesh, in_specs=placed, out_specs=P("tm", None, "space", None, None), check_vma=False
    )
```

```python
import functools

import jax
import jax.numpy as jnp
from jax import lax
from jax.experimental import pallas as pl
from jax.experimental.pallas import tpu as pltpu
from jax.sharding import PartitionSpec as P

MESH = pl.DeviceIdType.MESH
STEPS = 8
SPAN = 3
ROUNDS = SPAN + 1
GHOST = 4
FIRST = 2
PIECES = 2
ROW0 = 8


def kernel(
    tms, spaces,
    region_in, coef_in, cell_in, amp_in, out_ref,
    region_ref, coef_ref, cell_ref, amp_ref,
    u, v, co, hist, send, force, rows_hot, cols_hot, amps, pieces,
    local_sem, out_sem, amp_send, amp_recv, co_send, co_recv, plane_send, plane_recv,
):
    t, s = lax.axis_index("tm"), lax.axis_index("space")
    cz, nx, ny = region_in.shape
    own = GHOST + 1
    has = (s > 0, s < spaces - 1)
    beside = ({"space": s - 1}, {"space": s + 1})

    barrier = pltpu.get_barrier_semaphore()
    expected = 0
    partners = [(has[0], beside[0]), (has[1], beside[1])]
    for m in range(1, SPAN + 1):
        partners.append((t - m >= 0, {"tm": t - m}))
        partners.append((t + m < tms, {"tm": t + m}))
    for there, device in partners:
        @pl.when(there)
        def _(device=device):
            pl.semaphore_signal(barrier, inc=1, device_id=device, device_id_type=MESH)
        expected = expected + jnp.where(there, 1, 0)

    loads = [
        pltpu.make_async_copy(region_in, region_ref, local_sem.at[0]),
        pltpu.make_async_copy(coef_in, coef_ref, local_sem.at[1]),
        pltpu.make_async_copy(amp_in.at[0], amp_ref, local_sem.at[2]),
        pltpu.make_async_copy(cell_in, cell_ref, local_sem.at[3]),
    ]
    for load in loads:
        load.start()

    loads[0].wait()
    loads[1].wait()
    for z in range(cz):
        region = region_ref[z]
        value = jnp.zeros((nx, ny), jnp.float32)
        for i in range(coef_ref.shape[0]):
            value = jnp.where(region == i, coef_ref[i], value)
        co[own + z] = value
    zero_plane = jnp.zeros((nx, ny), jnp.float32)
    loads[2].wait()
    pl.semaphore_wait(barrier, expected)

    halves = (pl.ds(0, FIRST), pl.ds(FIRST, STEPS - FIRST))

    def amp_copy(m, part):
        return pltpu.make_async_remote_copy(
            amp_ref.at[halves[part]], amps.at[m - 1, halves[part]], amp_send.at[m - 1, part], amp_recv.at[m - 1, part],
            device_id={"tm": t + m}, device_id_type=MESH)

    @pl.when(t + SPAN < tms)
    def _():
        for part in range(2):
            amp_copy(SPAN, part).start()

    def co_copy(side, d):
        source = own + d if side == 0 else own + cz - 1 - d
        target = own + cz + d if side == 0 else own - 1 - d
        return pltpu.make_async_remote_copy(
            co.at[source], co.at[target], co_send.at[side, d], co_recv.at[1 - side, d],
            device_id=beside[side], device_id_type=MESH)

    def co_wait(side, d):
        target = own - 1 - d if side == 0 else own + cz + d
        return pltpu.make_async_remote_copy(
            co.at[target], co.at[target], co_send.at[side, d], co_recv.at[side, d],
            device_id=beside[side], device_id_type=MESH)

    for d in range(GHOST):
        for side in range(2):
            @pl.when(has[side])
            def _(side=side, d=d):
                co_copy(side, d).start()

    def plane_copy(r, k, side):
        return pltpu.make_async_remote_copy(
            send.at[r, k, side], hist.at[r, k, 1 - side], plane_send.at[r, k, side], plane_recv.at[r, k, 1 - side],
            device_id=beside[side], device_id_type=MESH)

    def plane_wait(r, k, side):
        return pltpu.make_async_remote_copy(
            send.at[r, k, side], hist.at[r, k, side], plane_send.at[r, k, side], plane_recv.at[r, k, side],
            device_id=beside[side], device_id_type=MESH)

    def send_planes(r, k):
        for side in range(2):
            @pl.when(has[side])
            def _(side=side):
                plane_copy(r, k, side).start()

    def await_planes(r, k):
        for side in range(2):
            @pl.when(has[side])
            def _(side=side):
                plane_wait(r, k, side).wait_recv()

    def clear_u(p, _):
        for i in range(2):
            u[i, p] = jnp.zeros(u.shape[2:], jnp.float32)
        return 0

    def clear_v(z, _):
        for i in range(2):
            v[i, z] = jnp.zeros(v.shape[2:], jnp.float32)
        return 0

    lax.fori_loop(0, u.shape[1], clear_u, 0)
    lax.fori_loop(0, cz, clear_v, 0)
    for m in range(1, SPAN + 1):
        @pl.when(t - m < 0)
        def _(m=m):
            amps[m - 1] = jnp.zeros(amps.shape[1:], jnp.float32)
    for side in range(2):
        @pl.when(jnp.logical_not(has[side]))
        def _(side=side):
            for d in range(GHOST):
                co[own - 1 - d if side == 0 else own + cz + d] = zero_plane

            def clear_hist(i, _):
                hist[i // STEPS, lax.rem(i, STEPS), side] = zero_plane
                return 0

            lax.fori_loop(0, ROUNDS * STEPS, clear_hist, 0)

    half = cz // 2 * nx
    loads[3].wait()

    def rows_block(i, _):
        row = lax.rem(cell_ref[...] // ny, half)
        rows = 64
        index = lax.broadcasted_iota(jnp.int32, (rows, row.shape[1]), 0) + i * rows
        rows_hot[pl.ds(pl.multiple_of(i * rows, rows), rows), :] = jnp.where(row == index, 1.0, 0.0).astype(jnp.bfloat16)
        return 0

    lax.fori_loop(0, half // 64, rows_block, 0)
    sources = cell_ref.shape[1]
    for i in range(sources // 128):
        cell = jnp.broadcast_to(cell_ref[:, i * 128:(i + 1) * 128], (128, 128)).T
        col = cell // (half * ny) * ny + lax.rem(cell, ny)
        col = jnp.concatenate([col] * (2 * ny // 128), axis=1)
        index = lax.broadcasted_iota(jnp.int32, col.shape, 1)
        cols_hot[i * 128:(i + 1) * 128, :] = jnp.where(col == index, 1.0, 0.0).astype(jnp.bfloat16)

    def split_amplitude(slot, value, part):
        for piece in range(PIECES):
            rounded = value.astype(jnp.bfloat16).astype(jnp.float32)
            pieces[slot, piece, halves[part], :] = rounded
            value = value - rounded

    def take_amplitude(m, part):
        @pl.when(t - m >= 0)
        def _():
            amp_copy(m, part).wait_recv()

        split_amplitude(SPAN - m, amps[m - 1, halves[part], :], part)

    def make_force(slot, n):
        total = None
        for piece in range(PIECES):
            a = pieces[slot, piece, pl.ds(n, 1), :].astype(jnp.bfloat16)
            part = jnp.dot(rows_hot[...] * a, cols_hot[...], preferred_element_type=jnp.float32)
            total = part if total is None else total + part
        for z in range(cz):
            at, side = z % (cz // 2) * nx, z // (cz // 2) * ny
            force[n % 2, z] = total[at:at + nx, side:side + ny]

    lane = lax.broadcasted_iota(jnp.int32, (nx, ny), 1)
    first_lane, last_lane = lane == 0, lane == ny - 1
    inner = pl.ds(ROW0, nx)

    def advance(field, now, later, p, speed, above, below, live, old):
        around = [x for x in (above, below) if x is not None]
        around = functools.reduce(jnp.add, around) if around else None
        if not live:
            return speed * around
        c = field[now, p, inner, :]
        beside_x = field[now, p, pl.ds(ROW0 - 1, nx), :] + field[now, p, pl.ds(ROW0 + 1, nx), :]
        left = jnp.where(first_lane, 0.0, pltpu.roll(c, 1, axis=1))
        right = jnp.where(last_lane, 0.0, pltpu.roll(c, ny - 1, axis=1))
        near = beside_x + (left + right)
        around = near if around is None else around + near
        base = c + c
        if old:
            base = base - field[later, p, inner, :]
        return base + speed * (around - 6.0 * c)

    def run_alone(r, k):
        now, later = (k - 1) % 2, k % 2
        depth = min(k, STEPS - k)

        def outside(z):
            return max(-z, z - cz + 1)

        def at(z):
            return u[now, own + z, inner, :] if outside(z) <= k - 1 else None

        for z in range(-depth, cz + depth):
            new = advance(u, now, later, own + z, co[own + z], at(z - 1), at(z + 1), outside(z) <= k - 1, outside(z) <= max(k - 2, 0))
            if 0 <= z < cz:
                new = new + force[(k - 1) % 2, z]
            u[later, own + z, inner, :] = new
            if k < STEPS and z == 0:
                send[r, k, 0] = new
            if k < STEPS and z == cz - 1:
                send[r, k, 1] = new

    def run_caused(r, k, planes):
        now, later = (k - 1) % 2, k % 2

        def inside(z):
            return min(z + 1, cz - z)

        def at(z):
            if z < 0:
                return hist[r, k - 1, 0]
            if z >= cz:
                return hist[r, k - 1, 1]
            return v[now, z, inner, :] if inside(z) <= k - 1 else None

        for z in planes:
            if inside(z) > k:
                continue
            new = advance(v, now, later, z, co[own + z], at(z - 1), at(z + 1), inside(z) <= k - 1, inside(z) <= k - 2)
            if k < STEPS:
                v[later, z, inner, :] = new
            if k >= STEPS - 1:
                whole = u[later, own + z, inner, :] + new
                u[later, own + z, inner, :] = whole
                if k == STEPS and z in (0, cz - 1):
                    send[lax.rem(r + 1, ROUNDS), 0, 0 if z == 0 else 1] = whole

    for part in range(2):
        split_amplitude(SPAN, amp_ref[halves[part], :], part)

    out_copies = [
        pltpu.make_async_copy(u.at[1 - i, pl.ds(own, cz), inner, :], out_ref.at[0, i], out_sem.at[i]) for i in range(2)
    ]

    def one_round(r, _):
        for m in range(1, SPAN):
            @pl.when(r == SPAN - m)
            def _(m=m):
                for part in range(2):
                    take_amplitude(m, part)

        for k in range(1, STEPS + 1):
            @pl.when(r == 0)
            def _(k=k):
                if k == 1:
                    take_amplitude(SPAN, 0)
                if k == FIRST + 1:
                    take_amplitude(SPAN, 1)
                if k == STEPS // 2:
                    for m in range(SPAN - 1, 0, -1):
                        @pl.when(t + m < tms)
                        def _(m=m):
                            for part in range(2):
                                amp_copy(m, part).start()
                if k <= GHOST:
                    for side in range(2):
                        @pl.when(has[side])
                        def _(side=side):
                            co_wait(side, k - 1).wait_recv()

            make_force(r, k - 1)
            run_alone(r, k)
            if k < STEPS:
                send_planes(r, k)
        for k in range(1, STEPS + 1):
            if k == 1:
                @pl.when(r > 0)
                def _():
                    await_planes(r, 0)
                    run_caused(r, 1, range(cz))

                @pl.when(r == 0)
                def _():
                    for z in (0, cz - 1):
                        v[1, z, inner, :] = zero_plane
            elif k < STEPS:
                await_planes(r, k - 1)
                run_caused(r, k, range(cz))
                if k == STEPS - 1:
                    @pl.when(r == SPAN)
                    def _():
                        out_copies[0].start()
            else:
                await_planes(r, k - 1)
                run_caused(r, k, (0, cz - 1))

                @pl.when(r < SPAN)
                def _():
                    send_planes(r + 1, 0)

                run_caused(r, k, range(1, cz - 1))
        return 0

    lax.fori_loop(0, ROUNDS, one_round, 0)

    out_copies[1].start()
    for m in range(1, SPAN + 1):
        @pl.when(t + m < tms)
        def _(m=m):
            for part in range(2):
                amp_copy(m, part).wait_send()
    for side in range(2):
        @pl.when(has[side])
        def _(side=side):
            for d in range(GHOST):
                co_copy(side, d).wait_send()

            def drain(i, _):
                plane_copy(i // STEPS, lax.rem(i, STEPS), side).wait_send()
                return 0

            lax.fori_loop(1, ROUNDS * STEPS, drain, 0)
    for copy in out_copies:
        copy.wait()


def solution(mesh):
    tms, spaces = mesh.shape["tm"], mesh.shape["space"]

    def shards(region_map, region_coef, source_cell, amplitude):
        cz, nx, ny = region_map.shape
        sources = source_cell.shape[0]
        planes = cz + 2 * GHOST + 2
        return pl.pallas_call(
            functools.partial(kernel, tms, spaces),
            out_shape=jax.ShapeDtypeStruct((1, 2, cz, nx, ny), jnp.float32),
            in_specs=[pl.BlockSpec(memory_space=pl.ANY)] * 4,
            out_specs=pl.BlockSpec(memory_space=pl.ANY),
            scratch_shapes=[
                pltpu.VMEM((cz, nx, ny), jnp.int32),
                pltpu.SMEM(region_coef.shape, jnp.float32),
                pltpu.VMEM((1, sources), jnp.int32),
                pltpu.VMEM((STEPS, sources), jnp.float32),
                pltpu.VMEM((2, planes, nx + 2 * ROW0, ny), jnp.float32),
                pltpu.VMEM((2, cz, nx + 2 * ROW0, ny), jnp.float32),
                pltpu.VMEM((planes, nx, ny), jnp.float32),
                pltpu.VMEM((ROUNDS, STEPS, 2, nx, ny), jnp.float32),
                pltpu.VMEM((ROUNDS, STEPS, 2, nx, ny), jnp.float32),
                pltpu.VMEM((2, cz, nx, ny), jnp.float32),
                pltpu.VMEM((cz // 2 * nx, sources), jnp.bfloat16),
                pltpu.VMEM((sources, 2 * ny), jnp.bfloat16),
                pltpu.VMEM((SPAN, STEPS, sources), jnp.float32),
                pltpu.VMEM((ROUNDS, PIECES, STEPS, sources), jnp.float32),
                pltpu.SemaphoreType.DMA((4,)),
                pltpu.SemaphoreType.DMA((2,)),
                pltpu.SemaphoreType.DMA((SPAN, 2)),
                pltpu.SemaphoreType.DMA((SPAN, 2)),
                pltpu.SemaphoreType.DMA((2, GHOST)),
                pltpu.SemaphoreType.DMA((2, GHOST)),
                pltpu.SemaphoreType.DMA((ROUNDS, STEPS, 2)),
                pltpu.SemaphoreType.DMA((ROUNDS, STEPS, 2)),
            ],
            compiler_params=pltpu.CompilerParams(
                collective_id=0, has_side_effects=True, vmem_limit_bytes=60 << 20
            ),
        )(region_map, region_coef, source_cell.reshape(1, sources), amplitude)

    placed = (P("space", None, None), P(), P("space"), P("tm", None, "space"))
    return jax.shard_map(
        shards, mesh=mesh, in_specs=placed, out_specs=P("tm", None, "space", None, None), check_vma=False
    )
```

```python
import functools

import jax
import jax.numpy as jnp
from jax import lax
from jax.experimental import pallas as pl
from jax.experimental.pallas import tpu as pltpu
from jax.sharding import PartitionSpec as P

MESH = pl.DeviceIdType.MESH
STEPS = 8
SPAN = 3
ROUNDS = SPAN + 1
GHOST = 4
FIRST = 2
PIECES = 2
ROW0 = 8


def kernel(
    tms, spaces,
    region_in, coef_in, cell_in, amp_in, out_ref,
    region_ref, coef_ref, cell_ref, amp_ref,
    u, v, co, hist, send, leak, first, through, force, rows_hot, cols_hot, amps, pieces,
    local_sem, amp_send, amp_recv, co_send, co_recv, plane_send, plane_recv,
):
    t, s = lax.axis_index("tm"), lax.axis_index("space")
    cz, nx, ny = region_in.shape
    own = GHOST + 1
    has = (s > 0, s < spaces - 1)
    beside = ({"space": s - 1}, {"space": s + 1})

    barrier = pltpu.get_barrier_semaphore()
    expected = 0
    partners = [(has[0], beside[0]), (has[1], beside[1])]
    for m in range(1, SPAN + 1):
        partners.append((t - m >= 0, {"tm": t - m}))
        partners.append((t + m < tms, {"tm": t + m}))
    for there, device in partners:
        @pl.when(there)
        def _(device=device):
            pl.semaphore_signal(barrier, inc=1, device_id=device, device_id_type=MESH)
        expected = expected + jnp.where(there, 1, 0)

    loads = [
        pltpu.make_async_copy(region_in, region_ref, local_sem.at[0]),
        pltpu.make_async_copy(coef_in, coef_ref, local_sem.at[1]),
        pltpu.make_async_copy(amp_in.at[0], amp_ref, local_sem.at[2]),
        pltpu.make_async_copy(cell_in, cell_ref, local_sem.at[3]),
    ]
    for load in loads:
        load.start()

    loads[0].wait()
    loads[1].wait()
    for z in range(cz):
        region = region_ref[z]
        value = jnp.zeros((nx, ny), jnp.float32)
        for i in range(coef_ref.shape[0]):
            value = jnp.where(region == i, coef_ref[i], value)
        co[own + z] = value
    zero_plane = jnp.zeros((nx, ny), jnp.float32)
    loads[2].wait()
    pl.semaphore_wait(barrier, expected)

    halves = (pl.ds(0, FIRST), pl.ds(FIRST, STEPS - FIRST))

    def amp_copy(m, part):
        return pltpu.make_async_remote_copy(
            amp_ref.at[halves[part]], amps.at[m - 1, halves[part]], amp_send.at[m - 1, part], amp_recv.at[m - 1, part],
            device_id={"tm": t + m}, device_id_type=MESH)

    @pl.when(t + SPAN < tms)
    def _():
        for part in range(2):
            amp_copy(SPAN, part).start()

    def co_copy(side, d):
        source = own + d if side == 0 else own + cz - 1 - d
        target = own + cz + d if side == 0 else own - 1 - d
        return pltpu.make_async_remote_copy(
            co.at[source], co.at[target], co_send.at[side, d], co_recv.at[1 - side, d],
            device_id=beside[side], device_id_type=MESH)

    def co_wait(side, d):
        target = own - 1 - d if side == 0 else own + cz + d
        return pltpu.make_async_remote_copy(
            co.at[target], co.at[target], co_send.at[side, d], co_recv.at[side, d],
            device_id=beside[side], device_id_type=MESH)

    for d in range(GHOST):
        for side in range(2):
            @pl.when(has[side])
            def _(side=side, d=d):
                co_copy(side, d).start()

    def plane_copy(r, k, side):
        return pltpu.make_async_remote_copy(
            send.at[r, k, side], hist.at[r, k, 1 - side], plane_send.at[r, k, side], plane_recv.at[r, k, 1 - side],
            device_id=beside[side], device_id_type=MESH)

    def plane_wait(r, k, side):
        return pltpu.make_async_remote_copy(
            send.at[r, k, side], hist.at[r, k, side], plane_send.at[r, k, side], plane_recv.at[r, k, side],
            device_id=beside[side], device_id_type=MESH)

    def send_planes(r, k):
        for side in range(2):
            @pl.when(has[side])
            def _(side=side):
                plane_copy(r, k, side).start()

    def await_planes(r, k):
        for side in range(2):
            @pl.when(has[side])
            def _(side=side):
                plane_wait(r, k, side).wait_recv()

    through[...] = functools.reduce(jnp.multiply, [co[own + z] for z in range(cz)])

    for side in range(2):
        first[side] = zero_plane

    def clear_u(p, _):
        for i in range(2):
            u[i, p] = jnp.zeros(u.shape[2:], jnp.float32)
        return 0

    def clear_v(z, _):
        for i in range(2):
            v[i, z] = jnp.zeros(v.shape[2:], jnp.float32)
        return 0

    lax.fori_loop(0, u.shape[1], clear_u, 0)
    lax.fori_loop(0, cz, clear_v, 0)
    for m in range(1, SPAN + 1):
        @pl.when(t - m < 0)
        def _(m=m):
            amps[m - 1] = jnp.zeros(amps.shape[1:], jnp.float32)
    for side in range(2):
        @pl.when(jnp.logical_not(has[side]))
        def _(side=side):
            for d in range(GHOST):
                co[own - 1 - d if side == 0 else own + cz + d] = zero_plane

            def clear_hist(i, _):
                hist[i // STEPS, lax.rem(i, STEPS), side] = zero_plane
                return 0

            lax.fori_loop(0, ROUNDS * STEPS, clear_hist, 0)

    half = cz // 2 * nx
    loads[3].wait()

    def rows_block(i, _):
        row = lax.rem(cell_ref[...] // ny, half)
        rows = 64
        index = lax.broadcasted_iota(jnp.int32, (rows, row.shape[1]), 0) + i * rows
        rows_hot[pl.ds(pl.multiple_of(i * rows, rows), rows), :] = jnp.where(row == index, 1.0, 0.0).astype(jnp.bfloat16)
        return 0

    lax.fori_loop(0, half // 64, rows_block, 0)
    sources = cell_ref.shape[1]
    for i in range(sources // 128):
        cell = jnp.broadcast_to(cell_ref[:, i * 128:(i + 1) * 128], (128, 128)).T
        col = cell // (half * ny) * ny + lax.rem(cell, ny)
        col = jnp.concatenate([col] * (2 * ny // 128), axis=1)
        index = lax.broadcasted_iota(jnp.int32, col.shape, 1)
        cols_hot[i * 128:(i + 1) * 128, :] = jnp.where(col == index, 1.0, 0.0).astype(jnp.bfloat16)

    def split_amplitude(slot, value, part):
        for piece in range(PIECES):
            rounded = value.astype(jnp.bfloat16).astype(jnp.float32)
            pieces[slot, piece, halves[part], :] = rounded
            value = value - rounded

    def take_amplitude(m, part):
        @pl.when(t - m >= 0)
        def _():
            amp_copy(m, part).wait_recv()

        split_amplitude(SPAN - m, amps[m - 1, halves[part], :], part)

    def make_force(slot, n):
        total = None
        for piece in range(PIECES):
            a = pieces[slot, piece, pl.ds(n, 1), :].astype(jnp.bfloat16)
            part = jnp.dot(rows_hot[...] * a, cols_hot[...], preferred_element_type=jnp.float32)
            total = part if total is None else total + part
        for z in range(cz):
            at, side = z % (cz // 2) * nx, z // (cz // 2) * ny
            force[n % 2, z] = total[at:at + nx, side:side + ny]

    lane = lax.broadcasted_iota(jnp.int32, (nx, ny), 1)
    first_lane, last_lane = lane == 0, lane == ny - 1
    inner = pl.ds(ROW0, nx)

    def advance(field, now, later, p, speed, above, below, live, old):
        around = [x for x in (above, below) if x is not None]
        around = functools.reduce(jnp.add, around) if around else None
        if not live:
            return speed * around
        c = field[now, p, inner, :]
        beside_x = field[now, p, pl.ds(ROW0 - 1, nx), :] + field[now, p, pl.ds(ROW0 + 1, nx), :]
        left = jnp.where(first_lane, 0.0, pltpu.roll(c, 1, axis=1))
        right = jnp.where(last_lane, 0.0, pltpu.roll(c, ny - 1, axis=1))
        near = beside_x + (left + right)
        around = near if around is None else around + near
        base = c + c
        if old:
            base = base - field[later, p, inner, :]
        return base + speed * (around - 6.0 * c)

    def run_alone(r, k, planes):
        now, later = (k - 1) % 2, k % 2

        def outside(z):
            return max(-z, z - cz + 1)

        def at(z):
            return u[now, own + z, inner, :] if outside(z) <= k - 1 else None

        for z in planes:
            new = advance(u, now, later, own + z, co[own + z], at(z - 1), at(z + 1), outside(z) <= k - 1, outside(z) <= max(k - 2, 0))
            if 0 <= z < cz:
                new = new + force[(k - 1) % 2, z]
            elif k == STEPS:
                leak[0 if z < 0 else 1] = new
                continue
            u[later, own + z, inner, :] = new
            if k < STEPS and z == 0:
                send[r, k, 0] = new
            if k < STEPS and z == cz - 1:
                send[r, k, 1] = new

    def run_caused(r, k, planes):
        now, later = (k - 1) % 2, k % 2

        def inside(z):
            return min(z + 1, cz - z)

        def at(z):
            if z < 0 or z >= cz:
                side = 0 if z < 0 else 1
                return hist[r, k - 1, side] if k > 1 else first[side]
            return v[now, z, inner, :] if inside(z) <= k - 1 else None

        for z in planes:
            if inside(z) > k:
                continue
            new = advance(v, now, later, z, co[own + z], at(z - 1), at(z + 1), inside(z) <= k - 1, inside(z) <= k - 2)
            if k < STEPS:
                v[later, z, inner, :] = new
            if k >= STEPS - 1:
                whole = u[later, own + z, inner, :] + new
                u[later, own + z, inner, :] = whole
                out_ref[0, k - STEPS + 1, z] = whole

    for part in range(2):
        split_amplitude(SPAN, amp_ref[halves[part], :], part)

    edges = (0, cz - 1)

    def one_round(r, _):
        @pl.when(r > 0)
        def _():
            await_planes(r, 0)
            for side in range(2):
                first[side] = hist[r, 0, side] + leak[side]

        for k in range(1, STEPS + 1):
            @pl.when(r == 0)
            def _(k=k):
                if k == FIRST + 1:
                    take_amplitude(SPAN, 1)
                if k == STEPS // 2:
                    for m in range(SPAN - 1, 0, -1):
                        @pl.when(t + m < tms)
                        def _(m=m):
                            for part in range(2):
                                amp_copy(m, part).start()
                if k <= GHOST:
                    for side in range(2):
                        @pl.when(has[side])
                        def _(side=side):
                            co_wait(side, k - 1).wait_recv()

            depth = min(k, STEPS + 1 - k)
            if k > 1:
                make_force(r, k - 1)
            run_alone(r, k, [z for z in range(-depth, cz + depth) if k > 1 or z not in edges])
            if 1 < k < STEPS:
                send_planes(r, k)

        following = lax.rem(r + 1, ROUNDS)
        for side in range(2):
            send[following, 0, side] = u[0, own + edges[side], inner, :] + through[...] * first[1 - side]

        @pl.when(r < SPAN)
        def _():
            send_planes(r + 1, 0)

        for k in range(1, STEPS + 1):
            if k == STEPS:
                for m in range(1, SPAN):
                    @pl.when(r + 1 == SPAN - m)
                    def _(m=m):
                        for part in range(2):
                            take_amplitude(m, part)

                @pl.when(r < SPAN)
                def _():
                    make_force(r + 1, 0)

            if k > 1:
                await_planes(r, k - 1)
            if k < STEPS:
                run_caused(r, k, range(cz))

        run_caused(r, STEPS, (0, 1, cz - 2, cz - 1))

        @pl.when(r < SPAN)
        def _():
            run_alone(r + 1, 1, edges)
            send_planes(r + 1, 1)

        run_caused(r, STEPS, range(2, cz - 2))
        return 0

    take_amplitude(SPAN, 0)
    make_force(0, 0)
    run_alone(0, 1, edges)
    send_planes(0, 1)
    lax.fori_loop(0, ROUNDS, one_round, 0)

    for m in range(1, SPAN + 1):
        @pl.when(t + m < tms)
        def _(m=m):
            for part in range(2):
                amp_copy(m, part).wait_send()
    for side in range(2):
        @pl.when(has[side])
        def _(side=side):
            for d in range(GHOST):
                co_copy(side, d).wait_send()

            def drain(i, _):
                plane_copy(i // STEPS, lax.rem(i, STEPS), side).wait_send()
                return 0

            lax.fori_loop(1, ROUNDS * STEPS, drain, 0)


def solution(mesh):
    tms, spaces = mesh.shape["tm"], mesh.shape["space"]

    def shards(region_map, region_coef, source_cell, amplitude):
        cz, nx, ny = region_map.shape
        sources = source_cell.shape[0]
        planes = cz + 2 * GHOST + 2
        return pl.pallas_call(
            functools.partial(kernel, tms, spaces),
            out_shape=pltpu.VMEM((1, 2, cz, nx, ny), jnp.float32),
            in_specs=[pl.BlockSpec(memory_space=pl.ANY)] * 4,
            out_specs=pl.BlockSpec(memory_space=pltpu.VMEM),
            scratch_shapes=[
                pltpu.VMEM((cz, nx, ny), jnp.int32),
                pltpu.SMEM(region_coef.shape, jnp.float32),
                pltpu.VMEM((1, sources), jnp.int32),
                pltpu.VMEM((STEPS, sources), jnp.float32),
                pltpu.VMEM((2, planes, nx + 2 * ROW0, ny), jnp.float32),
                pltpu.VMEM((2, cz, nx + 2 * ROW0, ny), jnp.float32),
                pltpu.VMEM((planes, nx, ny), jnp.float32),
                pltpu.VMEM((ROUNDS, STEPS, 2, nx, ny), jnp.float32),
                pltpu.VMEM((ROUNDS, STEPS, 2, nx, ny), jnp.float32),
                pltpu.VMEM((2, nx, ny), jnp.float32),
                pltpu.VMEM((2, nx, ny), jnp.float32),
                pltpu.VMEM((nx, ny), jnp.float32),
                pltpu.VMEM((2, cz, nx, ny), jnp.float32),
                pltpu.VMEM((cz // 2 * nx, sources), jnp.bfloat16),
                pltpu.VMEM((sources, 2 * ny), jnp.bfloat16),
                pltpu.VMEM((SPAN, STEPS, sources), jnp.float32),
                pltpu.VMEM((ROUNDS, PIECES, STEPS, sources), jnp.float32),
                pltpu.SemaphoreType.DMA((4,)),
                pltpu.SemaphoreType.DMA((SPAN, 2)),
                pltpu.SemaphoreType.DMA((SPAN, 2)),
                pltpu.SemaphoreType.DMA((2, GHOST)),
                pltpu.SemaphoreType.DMA((2, GHOST)),
                pltpu.SemaphoreType.DMA((ROUNDS, STEPS, 2)),
                pltpu.SemaphoreType.DMA((ROUNDS, STEPS, 2)),
            ],
            compiler_params=pltpu.CompilerParams(
                collective_id=0, has_side_effects=True, vmem_limit_bytes=60 << 20
            ),
        )(region_map, region_coef, source_cell.reshape(1, sources), amplitude)

    placed = (P("space", None, None), P(), P("space"), P("tm", None, "space"))
    return jax.shard_map(
        shards, mesh=mesh, in_specs=placed, out_specs=P("tm", None, "space", None, None), check_vma=False
    )
```

```python
import functools

import jax
import jax.numpy as jnp
from jax import lax
from jax.experimental import pallas as pl
from jax.experimental.pallas import tpu as pltpu
from jax.sharding import PartitionSpec as P

MESH = pl.DeviceIdType.MESH
STEPS = 8
SPAN = 3
ROUNDS = SPAN + 1
GHOST = 4
FIRST = 2
PIECES = 2
ROW0 = 8


def kernel(
    tms, spaces,
    region_in, coef_in, cell_in, amp_in, out_ref,
    region_ref, coef_ref, cell_ref, amp_ref,
    u, v, co, hist, send, leak, first, through, force, rows_hot, cols_hot, amps, pieces,
    local_sem, amp_send, amp_recv, co_send, co_recv, plane_send, plane_recv,
):
    t, s = lax.axis_index("tm"), lax.axis_index("space")
    cz, nx, ny = region_in.shape
    own = GHOST + 1
    has = (s > 0, s < spaces - 1)
    beside = ({"space": s - 1}, {"space": s + 1})

    barrier = pltpu.get_barrier_semaphore()
    expected = 0
    partners = [(has[0], beside[0]), (has[1], beside[1])]
    for m in range(1, SPAN + 1):
        partners.append((t - m >= 0, {"tm": t - m}))
        partners.append((t + m < tms, {"tm": t + m}))
    for there, device in partners:
        @pl.when(there)
        def _(device=device):
            pl.semaphore_signal(barrier, inc=1, device_id=device, device_id_type=MESH)
        expected = expected + jnp.where(there, 1, 0)

    loads = [
        pltpu.make_async_copy(region_in, region_ref, local_sem.at[0]),
        pltpu.make_async_copy(coef_in, coef_ref, local_sem.at[1]),
        pltpu.make_async_copy(amp_in.at[0], amp_ref, local_sem.at[2]),
        pltpu.make_async_copy(cell_in, cell_ref, local_sem.at[3]),
    ]
    for load in loads:
        load.start()

    loads[0].wait()
    loads[1].wait()
    for z in range(cz):
        region = region_ref[z]
        value = jnp.zeros((nx, ny), jnp.float32)
        for i in range(coef_ref.shape[0]):
            value = jnp.where(region == i, coef_ref[i], value)
        co[own + z] = value
    zero_plane = jnp.zeros((nx, ny), jnp.float32)
    loads[2].wait()
    pl.semaphore_wait(barrier, expected)

    halves = (pl.ds(0, FIRST), pl.ds(FIRST, STEPS - FIRST))

    def amp_copy(m, part):
        return pltpu.make_async_remote_copy(
            amp_ref.at[halves[part]], amps.at[m - 1, halves[part]], amp_send.at[m - 1, part], amp_recv.at[m - 1, part],
            device_id={"tm": t + m}, device_id_type=MESH)

    @pl.when(t + SPAN < tms)
    def _():
        for part in range(2):
            amp_copy(SPAN, part).start()

    def co_copy(side, d):
        source = own + d if side == 0 else own + cz - 1 - d
        target = own + cz + d if side == 0 else own - 1 - d
        return pltpu.make_async_remote_copy(
            co.at[source], co.at[target], co_send.at[side, d], co_recv.at[1 - side, d],
            device_id=beside[side], device_id_type=MESH)

    def co_wait(side, d):
        target = own - 1 - d if side == 0 else own + cz + d
        return pltpu.make_async_remote_copy(
            co.at[target], co.at[target], co_send.at[side, d], co_recv.at[side, d],
            device_id=beside[side], device_id_type=MESH)

    for d in range(GHOST):
        for side in range(2):
            @pl.when(has[side])
            def _(side=side, d=d):
                co_copy(side, d).start()

    def plane_copy(r, k, side):
        return pltpu.make_async_remote_copy(
            send.at[r, k, side], hist.at[r, k, 1 - side], plane_send.at[r, k, side], plane_recv.at[r, k, 1 - side],
            device_id=beside[side], device_id_type=MESH)

    def plane_wait(r, k, side):
        return pltpu.make_async_remote_copy(
            send.at[r, k, side], hist.at[r, k, side], plane_send.at[r, k, side], plane_recv.at[r, k, side],
            device_id=beside[side], device_id_type=MESH)

    def send_planes(r, k):
        for side in range(2):
            @pl.when(has[side])
            def _(side=side):
                plane_copy(r, k, side).start()

    def await_planes(r, k):
        for side in range(2):
            @pl.when(has[side])
            def _(side=side):
                plane_wait(r, k, side).wait_recv()

    through[...] = functools.reduce(jnp.multiply, [co[own + z] for z in range(cz)])

    for side in range(2):
        first[side] = zero_plane

    def clear_u(p, _):
        for i in range(2):
            u[i, p] = jnp.zeros(u.shape[2:], jnp.float32)
        return 0

    def clear_v(z, _):
        for i in range(2):
            v[i, z] = jnp.zeros(v.shape[2:], jnp.float32)
        return 0

    lax.fori_loop(0, u.shape[1], clear_u, 0)
    lax.fori_loop(0, cz, clear_v, 0)
    for m in range(1, SPAN + 1):
        @pl.when(t - m < 0)
        def _(m=m):
            amps[m - 1] = jnp.zeros(amps.shape[1:], jnp.float32)
    for side in range(2):
        @pl.when(jnp.logical_not(has[side]))
        def _(side=side):
            for d in range(GHOST):
                co[own - 1 - d if side == 0 else own + cz + d] = zero_plane

            def clear_hist(i, _):
                hist[i // STEPS, lax.rem(i, STEPS), side] = zero_plane
                return 0

            lax.fori_loop(0, ROUNDS * STEPS, clear_hist, 0)

    half = cz // 2 * nx
    loads[3].wait()

    def rows_block(i, _):
        row = lax.rem(cell_ref[...] // ny, half)
        rows = 64
        index = lax.broadcasted_iota(jnp.int32, (rows, row.shape[1]), 0) + i * rows
        rows_hot[pl.ds(pl.multiple_of(i * rows, rows), rows), :] = jnp.where(row == index, 1.0, 0.0).astype(jnp.bfloat16)
        return 0

    lax.fori_loop(0, half // 64, rows_block, 0)
    sources = cell_ref.shape[1]
    for i in range(sources // 128):
        cell = jnp.broadcast_to(cell_ref[:, i * 128:(i + 1) * 128], (128, 128)).T
        col = cell // (half * ny) * ny + lax.rem(cell, ny)
        col = jnp.concatenate([col] * (2 * ny // 128), axis=1)
        index = lax.broadcasted_iota(jnp.int32, col.shape, 1)
        cols_hot[i * 128:(i + 1) * 128, :] = jnp.where(col == index, 1.0, 0.0).astype(jnp.bfloat16)

    def split_amplitude(slot, value, part):
        for piece in range(PIECES):
            rounded = value.astype(jnp.bfloat16).astype(jnp.float32)
            pieces[slot, piece, halves[part], :] = rounded
            value = value - rounded

    def take_amplitude(m, part):
        @pl.when(t - m >= 0)
        def _():
            amp_copy(m, part).wait_recv()

        split_amplitude(SPAN - m, amps[m - 1, halves[part], :], part)

    def make_force(slot, n):
        total = None
        for piece in range(PIECES):
            a = pieces[slot, piece, pl.ds(n, 1), :].astype(jnp.bfloat16)
            part = jnp.dot(rows_hot[...] * a, cols_hot[...], preferred_element_type=jnp.float32)
            total = part if total is None else total + part
        for z in range(cz):
            at, side = z % (cz // 2) * nx, z // (cz // 2) * ny
            force[n % 2, z] = total[at:at + nx, side:side + ny]

    lane = lax.broadcasted_iota(jnp.int32, (nx, ny), 1)
    first_lane, last_lane = lane == 0, lane == ny - 1
    inner = pl.ds(ROW0, nx)

    def advance(field, now, later, p, speed, above, below, live, old):
        around = [x for x in (above, below) if x is not None]
        around = functools.reduce(jnp.add, around) if around else None
        if not live:
            return speed * around
        c = field[now, p, inner, :]
        beside_x = field[now, p, pl.ds(ROW0 - 1, nx), :] + field[now, p, pl.ds(ROW0 + 1, nx), :]
        left = jnp.where(first_lane, 0.0, pltpu.roll(c, 1, axis=1))
        right = jnp.where(last_lane, 0.0, pltpu.roll(c, ny - 1, axis=1))
        near = beside_x + (left + right)
        around = near if around is None else around + near
        base = c + c
        if old:
            base = base - field[later, p, inner, :]
        return base + speed * (around - 6.0 * c)

    def run_alone(r, k, planes):
        now, later = (k - 1) % 2, k % 2

        def outside(z):
            return max(-z, z - cz + 1)

        def at(z):
            return u[now, own + z, inner, :] if outside(z) <= k - 1 else None

        for z in planes:
            new = advance(u, now, later, own + z, co[own + z], at(z - 1), at(z + 1), outside(z) <= k - 1, outside(z) <= max(k - 2, 0))
            if 0 <= z < cz:
                new = new + force[(k - 1) % 2, z]
            elif k == STEPS:
                leak[0 if z < 0 else 1] = new
                continue
            u[later, own + z, inner, :] = new
            if k < STEPS and z == 0:
                send[r, k, 0] = new
            if k < STEPS and z == cz - 1:
                send[r, k, 1] = new

    def run_caused(r, k, planes):
        now, later = (k - 1) % 2, k % 2

        def inside(z):
            return min(z + 1, cz - z)

        def at(z):
            if z < 0 or z >= cz:
                side = 0 if z < 0 else 1
                return hist[r, k - 1, side] if k > 1 else first[side]
            return v[now, z, inner, :] if inside(z) <= k - 1 else None

        for z in planes:
            if inside(z) > k:
                continue
            new = advance(v, now, later, z, co[own + z], at(z - 1), at(z + 1), inside(z) <= k - 1, inside(z) <= k - 2)
            if k < STEPS:
                v[later, z, inner, :] = new
            if k >= STEPS - 1:
                whole = u[later, own + z, inner, :] + new
                u[later, own + z, inner, :] = whole
                out_ref[0, k - STEPS + 1, z] = whole

    for part in range(2):
        split_amplitude(SPAN, amp_ref[halves[part], :], part)

    edges = (0, cz - 1)

    def one_round(r, _):
        for k in range(1, STEPS + 1):
            @pl.when(r == 0)
            def _(k=k):
                if k == FIRST + 1:
                    take_amplitude(SPAN, 1)
                if k == STEPS // 2:
                    for m in range(SPAN - 1, 0, -1):
                        @pl.when(t + m < tms)
                        def _(m=m):
                            for part in range(2):
                                amp_copy(m, part).start()
                if k <= GHOST:
                    for side in range(2):
                        @pl.when(has[side])
                        def _(side=side):
                            co_wait(side, k - 1).wait_recv()

            if k == STEPS - 2:
                @pl.when(r > 0)
                def _():
                    await_planes(r, 0)
                    for side in range(2):
                        first[side] = hist[r, 0, side] + leak[side]

            depth = min(k, STEPS + 1 - k)
            if k > 1:
                make_force(r, k - 1)
            run_alone(r, k, [z for z in range(-depth, cz + depth) if k > 1 or z not in edges])
            if 1 < k < STEPS:
                send_planes(r, k)

        following = lax.rem(r + 1, ROUNDS)
        for side in range(2):
            send[following, 0, side] = u[0, own + edges[side], inner, :] + through[...] * first[1 - side]

        @pl.when(r < SPAN)
        def _():
            send_planes(r + 1, 0)

        for k in range(1, STEPS + 1):
            if k == STEPS:
                for m in range(1, SPAN):
                    @pl.when(r + 1 == SPAN - m)
                    def _(m=m):
                        for part in range(2):
                            take_amplitude(m, part)

                @pl.when(r < SPAN)
                def _():
                    make_force(r + 1, 0)

                run_caused(r, STEPS, range(1, cz - 1))

            if k > 1:
                await_planes(r, k - 1)
            if k < STEPS:
                run_caused(r, k, range(cz))

        run_caused(r, STEPS, edges)

        @pl.when(r < SPAN)
        def _():
            run_alone(r + 1, 1, edges)
            send_planes(r + 1, 1)

        return 0

    take_amplitude(SPAN, 0)
    make_force(0, 0)
    run_alone(0, 1, edges)
    send_planes(0, 1)
    lax.fori_loop(0, ROUNDS, one_round, 0)

    for m in range(1, SPAN + 1):
        @pl.when(t + m < tms)
        def _(m=m):
            for part in range(2):
                amp_copy(m, part).wait_send()
    for side in range(2):
        @pl.when(has[side])
        def _(side=side):
            for d in range(GHOST):
                co_copy(side, d).wait_send()

            def drain(i, _):
                plane_copy(i // STEPS, lax.rem(i, STEPS), side).wait_send()
                return 0

            lax.fori_loop(1, ROUNDS * STEPS, drain, 0)


def solution(mesh):
    tms, spaces = mesh.shape["tm"], mesh.shape["space"]

    def shards(region_map, region_coef, source_cell, amplitude):
        cz, nx, ny = region_map.shape
        sources = source_cell.shape[0]
        planes = cz + 2 * GHOST + 2
        return pl.pallas_call(
            functools.partial(kernel, tms, spaces),
            out_shape=pltpu.VMEM((1, 2, cz, nx, ny), jnp.float32),
            in_specs=[pl.BlockSpec(memory_space=pl.ANY)] * 4,
            out_specs=pl.BlockSpec(memory_space=pltpu.VMEM),
            scratch_shapes=[
                pltpu.VMEM((cz, nx, ny), jnp.int32),
                pltpu.SMEM(region_coef.shape, jnp.float32),
                pltpu.VMEM((1, sources), jnp.int32),
                pltpu.VMEM((STEPS, sources), jnp.float32),
                pltpu.VMEM((2, planes, nx + 2 * ROW0, ny), jnp.float32),
                pltpu.VMEM((2, cz, nx + 2 * ROW0, ny), jnp.float32),
                pltpu.VMEM((planes, nx, ny), jnp.float32),
                pltpu.VMEM((ROUNDS, STEPS, 2, nx, ny), jnp.float32),
                pltpu.VMEM((ROUNDS, STEPS, 2, nx, ny), jnp.float32),
                pltpu.VMEM((2, nx, ny), jnp.float32),
                pltpu.VMEM((2, nx, ny), jnp.float32),
                pltpu.VMEM((nx, ny), jnp.float32),
                pltpu.VMEM((2, cz, nx, ny), jnp.float32),
                pltpu.VMEM((cz // 2 * nx, sources), jnp.bfloat16),
                pltpu.VMEM((sources, 2 * ny), jnp.bfloat16),
                pltpu.VMEM((SPAN, STEPS, sources), jnp.float32),
                pltpu.VMEM((ROUNDS, PIECES, STEPS, sources), jnp.float32),
                pltpu.SemaphoreType.DMA((4,)),
                pltpu.SemaphoreType.DMA((SPAN, 2)),
                pltpu.SemaphoreType.DMA((SPAN, 2)),
                pltpu.SemaphoreType.DMA((2, GHOST)),
                pltpu.SemaphoreType.DMA((2, GHOST)),
                pltpu.SemaphoreType.DMA((ROUNDS, STEPS, 2)),
                pltpu.SemaphoreType.DMA((ROUNDS, STEPS, 2)),
            ],
            compiler_params=pltpu.CompilerParams(
                collective_id=0, has_side_effects=True, vmem_limit_bytes=60 << 20
            ),
        )(region_map, region_coef, source_cell.reshape(1, sources), amplitude)

    placed = (P("space", None, None), P(), P("space"), P("tm", None, "space"))
    return jax.shard_map(
        shards, mesh=mesh, in_specs=placed, out_specs=P("tm", None, "space", None, None), check_vma=False
    )
```
